32 devices in a mesh: groups: 2 (over x), pts: 16 (over z, y, core).
Axes of the slice: x: 2, y: 2, z: 4, core: 2. Of those that a mesh axis runs over, the one named last changes fastest.
Arguments:
- points: float32 [32, 8192], P(None, ('groups', 'pts')), parts along dimension 1, may hold values from -6 to 6
- lengthscales: float32 [32], replicated, may hold values from 1.4 to 3
- noise: float32 [8192], P(('groups', 'pts')), parts along dimension 0, may hold values from 0.2 to 1
- targets: float32 [32, 8192], P(None, ('groups', 'pts')), parts along dimension 1, may hold values from -6 to 6
Outputs:
- solution: float32 [32, 8192], P(None, ('groups', 'pts')), parts along dimension 1
- residual: float32 [32, 8192], P(None, ('groups', 'pts')), parts along dimension 1
The draws below stay inside these ranges and needn't reach their ends.
There are 2 independent parts, one for each index of `groups`. The reference program is written for one: setup_inputs(seed, part) draws one part's arguments, and reference() takes and returns one part's arrays. A program takes and returns all parts, laid end to end along the dimension named above; an argument that names none is the same for every part. Nothing has to cross between parts.
All inputs are finite; a program needn't handle non-finite values.
Results may differ from the reference program's by a relative error of at most 0.0045.
Values sent between devices are 32-bit elements; how exact they have to be, the bound alone decides.
A program may use at most 64 MiB of HBM per device.

```python
import math
import jax
import jax.numpy as jnp
from jax import lax

F = 32
RHS = 32
ROWS_DEV = 256
ITERS = 3
NPTS = 4096


def block_levels(key, dims, pieces, low, largest):
    level = 1.0
    for axis_at, blocks in pieces:
        steps = jax.random.uniform(jax.random.fold_in(jax.random.fold_in(key, 6), axis_at), (blocks,), jnp.float32, low / len(pieces), largest / len(pieces))
        level = level * jnp.repeat(jnp.exp(steps), dims[axis_at] // blocks).reshape((-1,) + (1,) * (len(dims) - 1 - axis_at))
    return level


def scatter_about(rng, extent, scale, bound, pieces=(), kind=jnp.bfloat16):
    array = jax.random.normal(rng, extent, jnp.float32) * scale
    if len(pieces) > 0:
        array = block_levels(rng, extent, pieces, -0.22, 0.18) * array
    return jnp.clip(array, min=-bound, max=bound).astype(kind)


def setup_inputs(seed: int = 0, part: int = 0) -> dict:
    streams_of = jax.random.split(jax.random.key(seed), 5)
    own_keys = jax.random.split(jax.random.fold_in(streams_of[4], part), 5)
    points = scatter_about(own_keys[0], (F, NPTS), 1.0, 6.0, ((1, 16),), jnp.float32)
    lengthscales = jnp.clip(jnp.exp(jax.random.uniform(streams_of[1], (F,), jnp.float32, math.log(1.4), math.log(3.0))), 1.4, 3.0)
    noise = jnp.clip(jnp.exp(math.log(1.0) - 1.609438 * jax.random.uniform(own_keys[2], (NPTS,), jnp.float32) ** block_levels(own_keys[2], (NPTS,), ((0, 16),), -0.2, 0.2)), 0.2, 1.0)
    targets = scatter_about(own_keys[3], (RHS, NPTS), 1.0, 6.0, ((1, 16),), jnp.float32)
    return dict(points=points, lengthscales=lengthscales, noise=noise, targets=targets)


root_five = math.sqrt(5.0)

def matern(left, right):
    cross = jnp.dot(left.T.astype(jnp.float32), right.astype(jnp.float32), precision=lax.Precision.HIGHEST, preferred_element_type=jnp.float32)
    dist2 = lax.optimization_barrier(jnp.sum(left * left, axis=0))[:, None] + lax.optimization_barrier(jnp.sum(right * right, axis=0))[None, :] - 2.0 * cross
    scaled_dist = root_five * jnp.sqrt(jnp.maximum(dist2, 0.0))
    return (1.0 + scaled_dist + scaled_dist * scaled_dist / 3.0) * jnp.exp(-scaled_dist)

def gram(left, right):
    return lax.dot_general(left.astype(jnp.float32), right.astype(jnp.float32), (((1,), (1,)), ((), ())), precision=lax.Precision.HIGHEST, preferred_element_type=jnp.float32)

def symmetric(matrix):
    return 0.5 * (matrix + matrix.T)

def spd_solve(matrix, right):
    lower = jnp.linalg.cholesky(matrix)
    return jax.scipy.linalg.cho_solve((lower, True), right)

def product(left, right):
    return jnp.dot(left.astype(jnp.float32), right.astype(jnp.float32), precision=lax.Precision.HIGHEST, preferred_element_type=jnp.float32)

def apply_kernel(scaled, direction, noise):

    def column_block(start):
        cols = lax.dynamic_slice_in_dim(scaled, start, ROWS_DEV, 1)
        return product(direction, matern(scaled, cols))
    starts = jnp.arange(NPTS // ROWS_DEV, dtype=jnp.int32) * ROWS_DEV
    blocks = lax.map(column_block, starts)
    image = jnp.transpose(blocks, (1, 0, 2)).reshape(direction.shape[0], NPTS)
    return image + noise[None, :] * direction

def reference(points, lengthscales, noise, targets):
    scaled = points / lengthscales[:, None]
    solution = jnp.zeros_like(targets)
    residual = targets
    direction = targets
    norm_now = symmetric(gram(residual, residual))
    for step in range(ITERS):
        image = apply_kernel(scaled, direction, noise)
        curv = symmetric(gram(direction, image))
        alpha = spd_solve(curv, norm_now)
        solution = solution + product(alpha.T, direction)
        residual = residual - product(alpha.T, image)
        if step + 1 < ITERS:
            norm_next = symmetric(gram(residual, residual))
            beta = spd_solve(norm_now, norm_next)
            direction = residual + product(beta.T, direction)
            norm_now = norm_next
    return (solution, residual)
```

```python
import functools

import jax
import jax.numpy as jnp
from jax import lax
from jax.experimental import pallas as pl
from jax.experimental.pallas import tpu as pltpu
from jax.sharding import PartitionSpec as P

ITERS = 3
MESH = pl.DeviceIdType.MESH
NT = (((1,), (1,)), ((), ()))
NN = (((1,), (0,)), ((), ()))
F32 = jnp.float32
BF16 = jnp.bfloat16


def mxu(left, right, dims):
    return lax.dot_general(left, right, dims, preferred_element_type=F32)


def split3(x):
    hi = x.astype(BF16)
    rest = x - hi.astype(F32)
    mid = rest.astype(BF16)
    low = (rest - mid.astype(F32)).astype(BF16)
    return hi, mid, low


def stack3(x):
    return jnp.concatenate(split3(x), axis=0)


def six_rows(stacked, rows):
    return jnp.concatenate([stacked, stacked[: 2 * rows], stacked[:rows]], axis=0)


def six_lanes(x):
    hi, mid, low = split3(x)
    wide = [hi, hi, hi, mid, mid, low]
    return jnp.concatenate([w.astype(F32) for w in wide], axis=1).astype(BF16)


def fold_gram(g, rows):
    r = rows
    total = g[2 * r :, :r] + g[r : 2 * r, r : 2 * r] + g[:r, 2 * r :]
    total = total + (g[r : 2 * r, :r] + g[:r, r : 2 * r])
    total = total + g[:r, :r]
    return 0.5 * (total + total.T)


def eliminate(systems, size):
    rows = lax.broadcasted_iota(jnp.int32, systems[0].shape, 0)
    for j in range(size):
        done = []
        for m in systems:
            col = jnp.broadcast_to(m[:, j : j + 1], m.shape)
            row = m[j : j + 1, :] / col[j : j + 1, :]
            done.append(jnp.where(rows == j, row, m - col * row))
        systems = done
    return [m[:, size : 2 * size] for m in systems]


def augmented(matrix, right):
    rows, size = matrix.shape
    pad = jnp.zeros((rows, 128 - 2 * size), F32)
    return jnp.concatenate([matrix, right, pad], axis=1)


def matern_tile(own, own_norm, feats):
    cross = mxu(own, six_rows(stack3(feats), feats.shape[0]), NN)
    norm = jnp.sum(feats * feats, axis=0, keepdims=True)
    d2 = own_norm + norm - 2.0 * cross
    x = jnp.maximum(5.0 * d2, 1e-30)
    t = x * lax.rsqrt(x)
    return (1.0 + t + x * (1.0 / 3.0)) * jnp.exp(-t)


def kernel(
    n, pts_ref, ls_ref, noise_ref, tgt_ref, sol_ref, res_ref,
    gbuf, qbuf, pbuf, kth, ktl, dst, qst, rbuf, own_t, own_n, q_own, d_own,
    acc_h, acc_l, gram,
    send1, send2, recv, send_p, recv_p,
):
    me = lax.axis_index("pts")
    chips = n // 2
    chip = me // 2
    core = lax.rem(me, 2)
    sibling = 2 * chip + 1 - core
    f, width = pts_ref.shape
    r = tgt_ref.shape[0]

    barrier = pltpu.get_barrier_semaphore()

    def greet(s, c):
        peer = lax.rem(me + s, n)
        pl.semaphore_signal(barrier, inc=1, device_id={"pts": peer}, device_id_type=MESH)
        return c

    lax.fori_loop(1, n, greet, 0)

    scaled = pts_ref[...] / ls_ref[...]
    gbuf[me, :f, :] = scaled
    gbuf[me, f:, :] = tgt_ref[...]
    scaled_t = scaled.T
    own_t[...] = six_lanes(scaled_t)
    own_n[...] = jnp.broadcast_to(jnp.sum(scaled_t * scaled_t, axis=1, keepdims=True), own_n.shape)
    d_own[...] = tgt_ref[...]

    pl.semaphore_wait(barrier, n - 1)

    def to_plane(rnd, buf, s):
        to = 2 * lax.rem(chip + s, chips) + core
        return pltpu.make_async_remote_copy(
            src_ref=buf.at[me], dst_ref=buf.at[me],
            send_sem=send1.at[rnd, s], recv_sem=recv.at[rnd, me],
            device_id={"pts": to}, device_id_type=MESH,
        )

    def to_sibling(rnd, buf, s, slot):
        return pltpu.make_async_remote_copy(
            src_ref=buf.at[slot], dst_ref=buf.at[slot],
            send_sem=send2.at[rnd, s], recv_sem=recv.at[rnd, slot],
            device_id={"pts": sibling}, device_id_type=MESH,
        )

    def source(s):
        return 2 * lax.rem(chip + chips - s, chips)

    def gather_start(rnd, buf):
        to_sibling(rnd, buf, 0, me).start()

        def one(s, c):
            to_plane(rnd, buf, s).start()
            return c

        lax.fori_loop(1, chips, one, 0)

    def gather_use(rnd, buf, use):
        use(me)
        to_sibling(rnd, buf, 0, sibling).wait_recv()
        use(sibling)

        def plane(s, c):
            slot = source(s) + core
            copy = to_sibling(rnd, buf, s, slot)
            copy.wait_recv()
            copy.start()
            use(slot)
            return c

        def other(s, c):
            slot = source(s) + 1 - core
            to_sibling(rnd, buf, s, slot).wait_recv()
            use(slot)
            return c

        lax.fori_loop(1, chips, plane, 0)
        lax.fori_loop(1, chips, other, 0)

    gather_start(0, gbuf)
    acc_h[...] = jnp.zeros_like(acc_h)
    acc_l[...] = jnp.zeros_like(acc_l)
    gram[...] = jnp.zeros_like(gram)

    def first(slot):
        tile = matern_tile(own_t[...], own_n[...], gbuf[slot, :f, :])
        high = tile.astype(BF16)
        low = (tile - high.astype(F32)).astype(BF16)
        kth[slot] = high
        ktl[slot] = low
        values = gbuf[slot, f:, :]
        rbuf[slot] = values
        stacked = stack3(values)
        dst[slot] = stacked
        gram[...] += mxu(stacked, stacked, NT)
        acc_h[...] += mxu(stacked, high, NT)
        acc_l[...] += mxu(stacked[: 2 * r], low, NT)

    gather_use(0, gbuf, first)
    rr = fold_gram(gram[...], r)
    eye = (
        lax.broadcasted_iota(jnp.int32, (r, r), 0) == lax.broadcasted_iota(jnp.int32, (r, r), 1)
    ).astype(F32)

    def image_own():
        h = acc_h[...]
        l = acc_l[...]
        return (h[2 * r :] + l[r:]) + (h[r : 2 * r] + l[:r]) + h[:r] + noise_ref[...] * d_own[...]

    solution = jnp.zeros((r, width), F32)
    for step in range(ITERS - 1):
        buf = qbuf.at[step]
        buf[me] = image_own()
        gather_start(step + 1, buf)
        gram[...] = jnp.zeros_like(gram)

        def curvature(slot, buf=buf):
            stacked = stack3(buf[slot])
            qst[slot] = stacked
            gram[...] += mxu(dst[slot], stacked, NT)

        gather_use(step + 1, buf, curvature)
        alpha, rr_inv = eliminate(
            [augmented(fold_gram(gram[...], r), rr), augmented(rr, eye)], r
        )
        alpha_t = six_lanes(alpha.T)
        solution = solution + mxu(alpha_t, six_rows(dst[me], r), NN)
        gram[...] = jnp.zeros_like(gram)

        def residuals(s, c, alpha_t=alpha_t):
            value = rbuf[s] - mxu(alpha_t, six_rows(qst[s], r), NN)
            rbuf[s] = value
            stacked = stack3(value)
            gram[...] += mxu(stacked, stacked, NT)
            return c

        lax.fori_loop(0, n, residuals, 0)
        rr_next = fold_gram(gram[...], r)
        beta = jnp.dot(rr_inv, rr_next, precision=lax.Precision.HIGHEST, preferred_element_type=F32)
        beta_t = six_lanes(beta.T)
        d_own[...] = rbuf[me] + mxu(beta_t, six_rows(dst[me], r), NN)
        acc_h[...] = jnp.zeros_like(acc_h)
        acc_l[...] = jnp.zeros_like(acc_l)

        def directions(s, c, beta_t=beta_t):
            value = rbuf[s] + mxu(beta_t, six_rows(dst[s], r), NN)
            stacked = stack3(value)
            dst[s] = stacked
            acc_h[...] += mxu(stacked, kth[s], NT)
            acc_l[...] += mxu(stacked[: 2 * r], ktl[s], NT)
            return c

        lax.fori_loop(0, n, directions, 0)
        rr = rr_next

    q_own[...] = image_own()
    q_stacked = stack3(q_own[...])
    g = mxu(dst[me], q_stacked, NT)
    partial = fold_gram(g, r)
    pbuf[me] = jnp.concatenate([partial, jnp.zeros((r, 128 - r), F32)], axis=1)

    def to_peer(s, slot):
        return pltpu.make_async_remote_copy(
            src_ref=pbuf.at[slot], dst_ref=pbuf.at[slot],
            send_sem=send_p.at[s], recv_sem=recv_p.at[slot],
            device_id={"pts": lax.rem(me + s, n)}, device_id_type=MESH,
        )

    def give(s, c):
        to_peer(s, me).start()
        return c

    lax.fori_loop(1, n, give, 0)

    def take(s, c):
        to_peer(s, lax.rem(me + n - s, n)).wait_recv()
        return c

    lax.fori_loop(1, n, take, 0)
    total = lax.fori_loop(0, n, lambda s, c: c + pbuf[s], jnp.zeros((r, 128), F32))
    (alpha,) = eliminate([augmented(total[:, :r], rr)], r)
    alpha_t = six_lanes(alpha.T)
    sol_ref[...] = solution + mxu(alpha_t, six_rows(dst[me], r), NN)
    res_ref[...] = rbuf[me] - mxu(alpha_t, six_rows(q_stacked, r), NN)

    def drain(s, c):
        for rnd in range(ITERS):
            buf = gbuf if rnd == 0 else qbuf.at[rnd - 1]
            to_plane(rnd, buf, s).wait_send()
            to_sibling(rnd, buf, s, me).wait_send()
        return c

    for rnd in range(ITERS):
        buf = gbuf if rnd == 0 else qbuf.at[rnd - 1]
        to_sibling(rnd, buf, 0, me).wait_send()
    lax.fori_loop(1, chips, drain, 0)

    def drain_peer(s, c):
        to_peer(s, me).wait_send()
        return c

    lax.fori_loop(1, n, drain_peer, 0)


def body(n, points, lengthscales, noise, targets):
    f, width = points.shape
    r = targets.shape[0]
    block = jax.ShapeDtypeStruct((r, width), F32)
    vmem = pl.BlockSpec(memory_space=pltpu.VMEM)
    return pl.pallas_call(
        functools.partial(kernel, n),
        out_shape=(block, block),
        in_specs=[vmem] * 4,
        out_specs=(vmem, vmem),
        scratch_shapes=[
            pltpu.VMEM((n, f + r, width), F32),
            pltpu.VMEM((ITERS - 1, n, r, width), F32),
            pltpu.VMEM((n, r, 128), F32),
            pltpu.VMEM((n, width, width), BF16),
            pltpu.VMEM((n, width, width), BF16),
            pltpu.VMEM((n, 3 * r, width), BF16),
            pltpu.VMEM((n, 3 * r, width), BF16),
            pltpu.VMEM((n, r, width), F32),
            pltpu.VMEM((width, 6 * f), BF16),
            pltpu.VMEM((width, width), F32),
            pltpu.VMEM((r, width), F32),
            pltpu.VMEM((r, width), F32),
            pltpu.VMEM((3 * r, width), F32),
            pltpu.VMEM((2 * r, width), F32),
            pltpu.VMEM((3 * r, 3 * r), F32),
            pltpu.SemaphoreType.DMA((ITERS, n // 2)),
            pltpu.SemaphoreType.DMA((ITERS, n // 2)),
            pltpu.SemaphoreType.DMA((ITERS, n)),
            pltpu.SemaphoreType.DMA((n,)),
            pltpu.SemaphoreType.DMA((n,)),
        ],
        compiler_params=pltpu.CompilerParams(
            collective_id=0, has_side_effects=True, vmem_limit_bytes=56 * 1024 * 1024
        ),
    )(points, lengthscales[:, None], noise[None, :], targets)


def solution(mesh):
    wide = P(None, ("groups", "pts"))
    return jax.shard_map(
        functools.partial(body, mesh.shape["pts"]),
        mesh=mesh,
        in_specs=(wide, P(), P(("groups", "pts")), wide),
        out_specs=(wide, wide),
        check_vma=False,
    )
```

```python
import functools

import jax
import jax.numpy as jnp
from jax import lax
from jax.experimental import pallas as pl
from jax.experimental.pallas import tpu as pltpu
from jax.sharding import PartitionSpec as P

ITERS = 3
MESH = pl.DeviceIdType.MESH
NT = (((1,), (1,)), ((), ()))
NN = (((1,), (0,)), ((), ()))
F32 = jnp.float32
BF16 = jnp.bfloat16


def mxu(left, right, dims):
    return lax.dot_general(left, right, dims, preferred_element_type=F32)


def split3(x):
    hi = x.astype(BF16)
    rest = x - hi.astype(F32)
    mid = rest.astype(BF16)
    low = (rest - mid.astype(F32)).astype(BF16)
    return hi, mid, low


def stack3(x):
    return jnp.concatenate(split3(x), axis=0)


def six_rows(stacked, rows):
    return jnp.concatenate([stacked, stacked[: 2 * rows], stacked[:rows]], axis=0)


def six_lanes(x):
    hi, mid, low = split3(x)
    wide = [hi, hi, hi, mid, mid, low]
    return jnp.concatenate([w.astype(F32) for w in wide], axis=1).astype(BF16)


def fold_gram(g, rows):
    r = rows
    total = g[2 * r :, :r] + g[r : 2 * r, r : 2 * r] + g[:r, 2 * r :]
    total = total + (g[r : 2 * r, :r] + g[:r, r : 2 * r])
    total = total + g[:r, :r]
    return 0.5 * (total + total.T)


def eliminate(systems, size):
    rows = lax.broadcasted_iota(jnp.int32, systems[0].shape, 0)
    for j in range(0, size, 2):
        i = j + 1
        done = []
        for m in systems:
            left = jnp.broadcast_to(m[:, j : j + 1], m.shape)
            right = jnp.broadcast_to(m[:, i : i + 1], m.shape)
            first, second = m[j : j + 1, :], m[i : i + 1, :]
            inv = 1.0 / left[j : j + 1, :]
            ratio = right[j : j + 1, :] * inv
            below = left[i : i + 1, :]
            schur = right[i : i + 1, :] - below * ratio
            second = (second - below * (first * inv)) / schur
            first = first * inv - ratio * second
            m = m - (left * first + right * second)
            done.append(jnp.where(rows == j, first, jnp.where(rows == i, second, m)))
        systems = done
    return [m[:, size : 2 * size] for m in systems]


def augmented(matrix, right):
    rows, size = matrix.shape
    pad = jnp.zeros((rows, 128 - 2 * size), F32)
    return jnp.concatenate([matrix, right, pad], axis=1)


def matern_tile(own, own_norm, feats):
    cross = mxu(own, six_rows(stack3(feats), feats.shape[0]), NN)
    norm = jnp.sum(feats * feats, axis=0, keepdims=True)
    d2 = own_norm + norm - 2.0 * cross
    x = jnp.maximum(5.0 * d2, 1e-30)
    t = x * lax.rsqrt(x)
    return (1.0 + t + x * (1.0 / 3.0)) * jnp.exp(-t)


def kernel(
    n, wide, pts_ref, ls_ref, noise_ref, tgt_ref, sol_ref, res_ref,
    gbuf, qbuf, pbuf, kth, ktl, dst, qst, rbuf, own_t, own_n, q_own, d_own,
    acc_h, acc_l, gram,
    send_z, send_y, send_k, recv, send_p, recv_p,
):
    me = lax.axis_index("pts")
    chips = n // 2
    deep = chips // wide
    chip = me // 2
    core = lax.rem(me, 2)
    sibling = 2 * chip + 1 - core
    z, y = chip // wide, lax.rem(chip, wide)

    def device(dz, dy):
        return 2 * (lax.rem(z + dz, deep) * wide + lax.rem(y + dy, wide)) + core
    f, width = pts_ref.shape
    r = tgt_ref.shape[0]

    barrier = pltpu.get_barrier_semaphore()

    def greet(s, c):
        peer = lax.rem(me + s, n)
        pl.semaphore_signal(barrier, inc=1, device_id={"pts": peer}, device_id_type=MESH)
        return c

    lax.fori_loop(1, n, greet, 0)

    scaled = pts_ref[...] / ls_ref[...]
    gbuf[me, :f, :] = scaled
    gbuf[me, f:, :] = tgt_ref[...]
    scaled_t = scaled.T
    own_t[...] = six_lanes(scaled_t)
    own_n[...] = jnp.broadcast_to(jnp.sum(scaled_t * scaled_t, axis=1, keepdims=True), own_n.shape)
    d_own[...] = tgt_ref[...]

    pl.semaphore_wait(barrier, n - 1)

    def to(rnd, buf, slot, peer, send):
        return pltpu.make_async_remote_copy(
            src_ref=buf.at[slot], dst_ref=buf.at[slot],
            send_sem=send, recv_sem=recv.at[rnd, slot],
            device_id={"pts": peer}, device_id_type=MESH,
        )

    def along_z(rnd, buf, dz):
        return to(rnd, buf, me, device(dz, 0), send_z.at[rnd, dz])

    def along_y(rnd, buf, dz, dy):
        return to(rnd, buf, device(deep - dz, 0), device(0, dy), send_y.at[rnd, dz, dy])

    def across(rnd, buf, dz, dy):
        slot = device(deep - dz, wide - dy)
        return to(rnd, buf, slot, sibling, send_k.at[rnd, dz, dy])

    def loop(begin, end, one):
        def run(s, c):
            one(s)
            return c

        lax.fori_loop(begin, end, run, 0)

    def gather_start(rnd, buf):
        loop(1, deep, lambda dz: along_z(rnd, buf, dz).start())
        for dy in range(1, wide):
            along_y(rnd, buf, 0, dy).start()
        across(rnd, buf, 0, 0).start()

    def gather_use(rnd, buf, use, batch):
        use([me])

        def lane(dz):
            copy = across(rnd, buf, dz, 0)
            copy.wait_recv()
            for dy in range(1, wide):
                along_y(rnd, buf, dz, dy).start()
            copy.start()
            use([device(deep - dz, 0)])

        loop(1, deep, lane)
        for dy in range(1, wide):

            def plane(dz, dy=dy):
                copy = across(rnd, buf, dz, dy)
                copy.wait_recv()
                copy.start()
                use([device(deep - dz, wide - dy)])

            loop(0, deep, plane)

        def other(s):
            slots = []
            for i in range(batch):
                at = s * batch + i
                slot = 2 * (lax.rem(z + deep - at // wide, deep) * wide + lax.rem(y + lax.rem(at, wide), wide)) + 1 - core
                to(rnd, buf, slot, sibling, send_k.at[rnd, 0, 0]).wait_recv()
                slots.append(slot)
            use(slots)

        loop(0, chips // batch, other)

    def lanes(parts):
        return parts[0] if len(parts) == 1 else jnp.concatenate(parts, axis=1)

    gather_start(0, gbuf)
    acc_h[...] = jnp.zeros_like(acc_h)
    acc_l[...] = jnp.zeros_like(acc_l)
    gram[...] = jnp.zeros_like(gram)

    def first(slots):
        stacks, highs, lows, values = [], [], [], [gbuf[slot, f:, :] for slot in slots]
        for slot, value in zip(slots, values):
            tile = matern_tile(own_t[...], own_n[...], gbuf[slot, :f, :])
            highs.append(tile.astype(BF16))
            lows.append((tile - highs[-1].astype(F32)).astype(BF16))
            stacks.append(stack3(value))
        stacked = lanes(stacks)
        gram[...] += mxu(stacked, stacked, NT)
        acc_h[...] += mxu(stacked, lanes(highs), NT)
        acc_l[...] += mxu(stacked[: 2 * r], lanes(lows), NT)
        for slot, value, high, low, stack in zip(slots, values, highs, lows, stacks):
            kth[slot] = high
            ktl[slot] = low
            rbuf[slot] = value
            dst[slot] = stack

    gather_use(0, gbuf, first, 2)
    rr = fold_gram(gram[...], r)
    eye = (
        lax.broadcasted_iota(jnp.int32, (r, r), 0) == lax.broadcasted_iota(jnp.int32, (r, r), 1)
    ).astype(F32)

    def image_own():
        h = acc_h[...]
        l = acc_l[...]
        return (h[2 * r :] + l[r:]) + (h[r : 2 * r] + l[:r]) + h[:r] + noise_ref[...] * d_own[...]

    solution = jnp.zeros((r, width), F32)
    for step in range(ITERS - 1):
        buf = qbuf.at[step]
        buf[me] = image_own()
        gather_start(step + 1, buf)
        gram[...] = jnp.zeros_like(gram)

        def curvature(slots, buf=buf):
            stacks = [stack3(buf[slot]) for slot in slots]
            gram[...] += mxu(lanes([dst[slot] for slot in slots]), lanes(stacks), NT)
            for slot, stack in zip(slots, stacks):
                qst[slot] = stack

        gather_use(step + 1, buf, curvature, 4)
        alpha, rr_inv = eliminate(
            [augmented(fold_gram(gram[...], r), rr), augmented(rr, eye)], r
        )
        alpha_t = six_lanes(alpha.T)
        solution = solution + mxu(alpha_t, six_rows(dst[me], r), NN)
        gram[...] = jnp.zeros_like(gram)

        def residuals(s, alpha_t=alpha_t):
            slots = [s * 4 + i for i in range(4)]
            value = lanes([rbuf[slot] for slot in slots]) - mxu(
                alpha_t, six_rows(lanes([qst[slot] for slot in slots]), r), NN
            )
            stacked = stack3(value)
            gram[...] += mxu(stacked, stacked, NT)
            for i, slot in enumerate(slots):
                rbuf[slot] = value[:, i * width : (i + 1) * width]

        loop(0, n // 4, residuals)
        rr_next = fold_gram(gram[...], r)
        beta = jnp.dot(rr_inv, rr_next, precision=lax.Precision.HIGHEST, preferred_element_type=F32)
        beta_t = six_lanes(beta.T)
        d_own[...] = rbuf[me] + mxu(beta_t, six_rows(dst[me], r), NN)
        acc_h[...] = jnp.zeros_like(acc_h)
        acc_l[...] = jnp.zeros_like(acc_l)

        def directions(s, beta_t=beta_t):
            slots = [s * 4 + i for i in range(4)]
            value = lanes([rbuf[slot] for slot in slots]) + mxu(
                beta_t, six_rows(lanes([dst[slot] for slot in slots]), r), NN
            )
            stacked = stack3(value)
            acc_h[...] += mxu(stacked, lanes([kth[slot] for slot in slots]), NT)
            acc_l[...] += mxu(stacked[: 2 * r], lanes([ktl[slot] for slot in slots]), NT)
            for i, slot in enumerate(slots):
                dst[slot] = stacked[:, i * width : (i + 1) * width]

        loop(0, n // 4, directions)
        rr = rr_next

    q_own[...] = image_own()
    q_stacked = stack3(q_own[...])
    g = mxu(dst[me], q_stacked, NT)
    partial = fold_gram(g, r)
    pbuf[me] = jnp.concatenate([partial, jnp.zeros((r, 128 - r), F32)], axis=1)

    def to_peer(s, slot):
        return pltpu.make_async_remote_copy(
            src_ref=pbuf.at[slot], dst_ref=pbuf.at[slot],
            send_sem=send_p.at[s], recv_sem=recv_p.at[slot],
            device_id={"pts": lax.rem(me + s, n)}, device_id_type=MESH,
        )

    def give(s, c):
        to_peer(s, me).start()
        return c

    lax.fori_loop(1, n, give, 0)

    def take(s, c):
        to_peer(s, lax.rem(me + n - s, n)).wait_recv()
        return c

    lax.fori_loop(1, n, take, 0)
    total = lax.fori_loop(0, n, lambda s, c: c + pbuf[s], jnp.zeros((r, 128), F32))
    (alpha,) = eliminate([augmented(total[:, :r], rr)], r)
    alpha_t = six_lanes(alpha.T)
    sol_ref[...] = solution + mxu(alpha_t, six_rows(dst[me], r), NN)
    res_ref[...] = rbuf[me] - mxu(alpha_t, six_rows(q_stacked, r), NN)

    for rnd in range(ITERS):
        buf = gbuf if rnd == 0 else qbuf.at[rnd - 1]

        def drain(dz, rnd=rnd, buf=buf):
            for dy in range(wide):
                if dy > 0:
                    along_y(rnd, buf, dz, dy).wait_send()
                across(rnd, buf, dz, dy).wait_send()

        loop(0, deep, drain)
        loop(1, deep, lambda dz, rnd=rnd, buf=buf: along_z(rnd, buf, dz).wait_send())

    def drain_peer(s, c):
        to_peer(s, me).wait_send()
        return c

    lax.fori_loop(1, n, drain_peer, 0)


def body(n, points, lengthscales, noise, targets):
    f, width = points.shape
    r = targets.shape[0]
    block = jax.ShapeDtypeStruct((r, width), F32)
    chips = n // 2
    wide = 2 if chips % 2 == 0 and chips <= 8 else 1
    deep = chips // wide
    vmem = pl.BlockSpec(memory_space=pltpu.VMEM)
    return pl.pallas_call(
        functools.partial(kernel, n, wide),
        out_shape=(block, block),
        in_specs=[vmem] * 4,
        out_specs=(vmem, vmem),
        scratch_shapes=[
            pltpu.VMEM((n, f + r, width), F32),
            pltpu.VMEM((ITERS - 1, n, r, width), F32),
            pltpu.VMEM((n, r, 128), F32),
            pltpu.VMEM((n, width, width), BF16),
            pltpu.VMEM((n, width, width), BF16),
            pltpu.VMEM((n, 3 * r, width), BF16),
            pltpu.VMEM((n, 3 * r, width), BF16),
            pltpu.VMEM((n, r, width), F32),
            pltpu.VMEM((width, 6 * f), BF16),
            pltpu.VMEM((width, width), F32),
            pltpu.VMEM((r, width), F32),
            pltpu.VMEM((r, width), F32),
            pltpu.VMEM((3 * r, width), F32),
            pltpu.VMEM((2 * r, width), F32),
            pltpu.VMEM((3 * r, 3 * r), F32),
            pltpu.SemaphoreType.DMA((ITERS, deep)),
            pltpu.SemaphoreType.DMA((ITERS, deep, wide)),
            pltpu.SemaphoreType.DMA((ITERS, deep, wide)),
            pltpu.SemaphoreType.DMA((ITERS, n)),
            pltpu.SemaphoreType.DMA((n,)),
            pltpu.SemaphoreType.DMA((n,)),
        ],
        compiler_params=pltpu.CompilerParams(
            collective_id=0, has_side_effects=True, vmem_limit_bytes=56 * 1024 * 1024
        ),
    )(points, lengthscales[:, None], noise[None, :], targets)


def solution(mesh):
    wide = P(None, ("groups", "pts"))
    return jax.shard_map(
        functools.partial(body, mesh.shape["pts"]),
        mesh=mesh,
        in_specs=(wide, P(), P(("groups", "pts")), wide),
        out_specs=(wide, wide),
        check_vma=False,
    )
```

```python
import functools

import jax
import jax.numpy as jnp
from jax import lax
from jax.experimental import pallas as pl
from jax.experimental.pallas import tpu as pltpu
from jax.sharding import PartitionSpec as P

ITERS = 3
MESH = pl.DeviceIdType.MESH
NT = (((1,), (1,)), ((), ()))
NN = (((1,), (0,)), ((), ()))
F32 = jnp.float32
BF16 = jnp.bfloat16


def mxu(left, right, dims):
    return lax.dot_general(left, right, dims, preferred_element_type=F32)


def split3(x):
    hi = x.astype(BF16)
    rest = x - hi.astype(F32)
    mid = rest.astype(BF16)
    low = (rest - mid.astype(F32)).astype(BF16)
    return hi, mid, low


def stack3(x):
    return jnp.concatenate(split3(x), axis=0)


def six_rows(stacked, rows):
    return jnp.concatenate([stacked, stacked[: 2 * rows], stacked[:rows]], axis=0)


def six_lanes(x):
    hi, mid, low = split3(x)
    wide = [hi, hi, hi, mid, mid, low]
    return jnp.concatenate([w.astype(F32) for w in wide], axis=1).astype(BF16)


def fold_gram(g, rows):
    r = rows
    total = g[2 * r :, :r] + g[r : 2 * r, r : 2 * r] + g[:r, 2 * r :]
    total = total + (g[r : 2 * r, :r] + g[:r, r : 2 * r])
    total = total + g[:r, :r]
    return 0.5 * (total + total.T)


def eliminate(systems, size):
    rows = lax.broadcasted_iota(jnp.int32, systems[0].shape, 0)
    for j in range(0, size, 2):
        i = j + 1
        done = []
        for m in systems:
            left = jnp.broadcast_to(m[:, j : j + 1], m.shape)
            right = jnp.broadcast_to(m[:, i : i + 1], m.shape)
            first, second = m[j : j + 1, :], m[i : i + 1, :]
            inv = 1.0 / left[j : j + 1, :]
            ratio = right[j : j + 1, :] * inv
            below = left[i : i + 1, :]
            schur = right[i : i + 1, :] - below * ratio
            second = (second - below * (first * inv)) / schur
            first = first * inv - ratio * second
            m = m - (left * first + right * second)
            done.append(jnp.where(rows == j, first, jnp.where(rows == i, second, m)))
        systems = done
    return [m[:, size : 2 * size] for m in systems]


def augmented(matrix, right):
    rows, size = matrix.shape
    pad = jnp.zeros((rows, 128 - 2 * size), F32)
    return jnp.concatenate([matrix, right, pad], axis=1)


def matern_tile(own, own_norm, feats):
    cross = mxu(own, six_rows(stack3(feats), feats.shape[0]), NN)
    norm = jnp.sum(feats * feats, axis=0, keepdims=True)
    d2 = own_norm + norm - 2.0 * cross
    x = jnp.maximum(5.0 * d2, 1e-30)
    t = x * lax.rsqrt(x)
    return (1.0 + t + x * (1.0 / 3.0)) * jnp.exp(-t)


def kernel(
    n, wide, pts_ref, ls_ref, noise_ref, tgt_ref, sol_ref, res_ref,
    gbuf, qbuf, pbuf, kth, ktl, dst, qst, rbuf, own_t, own_n, q_own,
    acc_h, acc_l, gram,
    send_z, send_y, send_k, recv, send_p, recv_p,
):
    me = lax.axis_index("pts")
    chips = n // 2
    deep = chips // wide
    chip = me // 2
    core = lax.rem(me, 2)
    sibling = 2 * chip + 1 - core
    z, y = chip // wide, lax.rem(chip, wide)

    def device(dz, dy):
        return 2 * (lax.rem(z + dz, deep) * wide + lax.rem(y + dy, wide)) + core
    f, width = pts_ref.shape
    r = tgt_ref.shape[0]

    barrier = pltpu.get_barrier_semaphore()

    def greet(s, c):
        peer = lax.rem(me + s, n)
        pl.semaphore_signal(barrier, inc=1, device_id={"pts": peer}, device_id_type=MESH)
        return c

    lax.fori_loop(1, n, greet, 0)

    scaled = pts_ref[...] / jnp.broadcast_to(ls_ref[...], (f, f)).T[:, :1]
    gbuf[me, :f, :] = scaled
    gbuf[me, f:, :] = tgt_ref[...]
    scaled_t = scaled.T
    own_t[...] = six_lanes(scaled_t)
    own_n[...] = jnp.broadcast_to(jnp.sum(scaled_t * scaled_t, axis=1, keepdims=True), own_n.shape)

    pl.semaphore_wait(barrier, n - 1)

    def to(rnd, buf, slot, peer, send):
        return pltpu.make_async_remote_copy(
            src_ref=buf.at[slot], dst_ref=buf.at[slot],
            send_sem=send, recv_sem=recv.at[rnd, slot],
            device_id={"pts": peer}, device_id_type=MESH,
        )

    def along_z(rnd, buf, dz):
        return to(rnd, buf, me, device(dz, 0), send_z.at[rnd, dz])

    def along_y(rnd, buf, dz, dy):
        return to(rnd, buf, device(deep - dz, 0), device(0, dy), send_y.at[rnd, dz, dy])

    def across(rnd, buf, dz, dy):
        slot = device(deep - dz, wide - dy)
        return to(rnd, buf, slot, sibling, send_k.at[rnd, dz, dy])

    def loop(begin, end, one):
        def run(s, c):
            one(s)
            return c

        lax.fori_loop(begin, end, run, 0)

    def gather_start(rnd, buf):
        loop(1, deep, lambda dz: along_z(rnd, buf, dz).start())
        for dy in range(1, wide):
            along_y(rnd, buf, 0, dy).start()
        across(rnd, buf, 0, 0).start()

    def gather_use(rnd, buf, use, batch):
        use([me])

        def lane(dz):
            copy = across(rnd, buf, dz, 0)
            copy.wait_recv()
            for dy in range(1, wide):
                along_y(rnd, buf, dz, dy).start()
            copy.start()
            use([device(deep - dz, 0)])

        loop(1, deep, lane)
        for dy in range(1, wide):

            def plane(dz, dy=dy):
                copy = across(rnd, buf, dz, dy)
                copy.wait_recv()
                copy.start()
                use([device(deep - dz, wide - dy)])

            loop(0, deep, plane)

        def other(s):
            slots = []
            for i in range(batch):
                at = s * batch + i
                slot = 2 * (lax.rem(z + deep - at // wide, deep) * wide + lax.rem(y + lax.rem(at, wide), wide)) + 1 - core
                to(rnd, buf, slot, sibling, send_k.at[rnd, 0, 0]).wait_recv()
                slots.append(slot)
            use(slots)

        loop(0, chips // batch, other)

    def lanes(parts):
        return parts[0] if len(parts) == 1 else jnp.concatenate(parts, axis=1)

    gather_start(0, gbuf)
    acc_h[...] = jnp.zeros_like(acc_h)
    acc_l[...] = jnp.zeros_like(acc_l)
    gram[...] = jnp.zeros_like(gram)

    def first(slots):
        stacks, highs, lows, values = [], [], [], [gbuf[slot, f:, :] for slot in slots]
        for slot, value in zip(slots, values):
            tile = matern_tile(own_t[...], own_n[...], gbuf[slot, :f, :])
            highs.append(tile.astype(BF16))
            lows.append((tile - highs[-1].astype(F32)).astype(BF16))
            stacks.append(stack3(value))
        stacked = lanes(stacks)
        gram[...] += mxu(stacked, stacked, NT)
        acc_h[...] += mxu(stacked, lanes(highs), NT)
        acc_l[...] += mxu(stacked[: 2 * r], lanes(lows), NT)
        for slot, value, high, low, stack in zip(slots, values, highs, lows, stacks):
            kth[slot] = high
            ktl[slot] = low
            rbuf[slot] = value
            dst[slot] = stack

    gather_use(0, gbuf, first, 2)
    rr = fold_gram(gram[...], r)
    eye = (
        lax.broadcasted_iota(jnp.int32, (r, r), 0) == lax.broadcasted_iota(jnp.int32, (r, r), 1)
    ).astype(F32)

    def operator(own):
        h = acc_h[...]
        l = acc_l[...]
        return (h[2 * r :] + l[r:]) + (h[r : 2 * r] + l[:r]) + h[:r] + noise_ref[...] * own

    solution = jnp.zeros((r, width), F32)
    image_r = operator(tgt_ref[...])
    q_own[...] = image_r
    for step in range(ITERS - 1):
        buf = qbuf.at[step]
        buf[me] = q_own[...]
        gather_start(step + 1, buf)
        if step > 0:

            def directions(s, beta_t=beta_t):
                slots = [s * 4 + i for i in range(4)]
                value = lanes([rbuf[slot] for slot in slots]) + mxu(
                    beta_t, six_rows(lanes([dst[slot] for slot in slots]), r), NN
                )
                stacked = stack3(value)
                for i, slot in enumerate(slots):
                    dst[slot] = stacked[:, i * width : (i + 1) * width]

            loop(0, n // 4, directions)
        gram[...] = jnp.zeros_like(gram)
        acc_h[...] = jnp.zeros_like(acc_h)
        acc_l[...] = jnp.zeros_like(acc_l)

        def curvature(slots, buf=buf):
            stacks = [stack3(buf[slot]) for slot in slots]
            stacked = lanes(stacks)
            gram[...] += mxu(lanes([dst[slot] for slot in slots]), stacked, NT)
            acc_h[...] += mxu(stacked, lanes([kth[slot] for slot in slots]), NT)
            acc_l[...] += mxu(stacked[: 2 * r], lanes([ktl[slot] for slot in slots]), NT)
            for slot, stack in zip(slots, stacks):
                qst[slot] = stack

        gather_use(step + 1, buf, curvature, 4)
        alpha, rr_inv = eliminate(
            [augmented(fold_gram(gram[...], r), rr), augmented(rr, eye)], r
        )
        alpha_t = six_lanes(alpha.T)
        solution = solution + mxu(alpha_t, six_rows(dst[me], r), NN)
        image_q = operator(q_own[...])
        image_r = image_r - mxu(alpha_t, six_rows(stack3(image_q), r), NN)
        gram[...] = jnp.zeros_like(gram)

        def residuals(s, alpha_t=alpha_t):
            slots = [s * 4 + i for i in range(4)]
            value = lanes([rbuf[slot] for slot in slots]) - mxu(
                alpha_t, six_rows(lanes([qst[slot] for slot in slots]), r), NN
            )
            stacked = stack3(value)
            gram[...] += mxu(stacked, stacked, NT)
            for i, slot in enumerate(slots):
                rbuf[slot] = value[:, i * width : (i + 1) * width]

        loop(0, n // 4, residuals)
        rr_next = fold_gram(gram[...], r)
        beta = jnp.dot(rr_inv, rr_next, precision=lax.Precision.HIGHEST, preferred_element_type=F32)
        beta_t = six_lanes(beta.T)
        q_own[...] = image_r + mxu(beta_t, six_rows(qst[me], r), NN)
        rr = rr_next

    dst[me] = stack3(rbuf[me] + mxu(beta_t, six_rows(dst[me], r), NN))
    q_stacked = stack3(q_own[...])
    g = mxu(dst[me], q_stacked, NT)
    partial = fold_gram(g, r)
    piece = pbuf.shape[1]
    pbuf[me] = jnp.concatenate([partial[i : i + piece] for i in range(0, r, piece)], axis=1)

    def to_peer(s, slot):
        return pltpu.make_async_remote_copy(
            src_ref=pbuf.at[slot], dst_ref=pbuf.at[slot],
            send_sem=send_p.at[s], recv_sem=recv_p.at[slot],
            device_id={"pts": lax.rem(me + s, n)}, device_id_type=MESH,
        )

    def give(s, c):
        to_peer(s, me).start()
        return c

    lax.fori_loop(1, n, give, 0)

    def take(s, c):
        to_peer(s, lax.rem(me + n - s, n)).wait_recv()
        return c

    lax.fori_loop(1, n, take, 0)
    total = lax.fori_loop(0, n, lambda s, c: c + pbuf[s], jnp.zeros((piece, 128), F32))
    total = jnp.concatenate([total[:, i : i + r] for i in range(0, 128, r)], axis=0)
    (alpha,) = eliminate([augmented(total, rr)], r)
    alpha_t = six_lanes(alpha.T)
    sol_ref[...] = solution + mxu(alpha_t, six_rows(dst[me], r), NN)
    res_ref[...] = rbuf[me] - mxu(alpha_t, six_rows(q_stacked, r), NN)

    for rnd in range(ITERS):
        buf = gbuf if rnd == 0 else qbuf.at[rnd - 1]

        def drain(dz, rnd=rnd, buf=buf):
            for dy in range(wide):
                if dy > 0:
                    along_y(rnd, buf, dz, dy).wait_send()
                across(rnd, buf, dz, dy).wait_send()

        loop(0, deep, drain)
        loop(1, deep, lambda dz, rnd=rnd, buf=buf: along_z(rnd, buf, dz).wait_send())

    def drain_peer(s, c):
        to_peer(s, me).wait_send()
        return c

    lax.fori_loop(1, n, drain_peer, 0)


def body(n, points, lengthscales, noise, targets):
    f, width = points.shape
    r = targets.shape[0]
    block = jax.ShapeDtypeStruct((r, width), F32)
    chips = n // 2
    wide = 2 if chips % 2 == 0 and chips <= 8 else 1
    deep = chips // wide
    vmem = pl.BlockSpec(memory_space=pltpu.VMEM)
    return pl.pallas_call(
        functools.partial(kernel, n, wide),
        out_shape=(block, block),
        in_specs=[vmem] * 4,
        out_specs=(vmem, vmem),
        scratch_shapes=[
            pltpu.VMEM((n, f + r, width), F32),
            pltpu.VMEM((ITERS - 1, n, r, width), F32),
            pltpu.VMEM((n, r * r // 128, 128), F32),
            pltpu.VMEM((n, width, width), BF16),
            pltpu.VMEM((n, width, width), BF16),
            pltpu.VMEM((n, 3 * r, width), BF16),
            pltpu.VMEM((n, 3 * r, width), BF16),
            pltpu.VMEM((n, r, width), F32),
            pltpu.VMEM((width, 6 * f), BF16),
            pltpu.VMEM((width, width), F32),
            pltpu.VMEM((r, width), F32),
            pltpu.VMEM((3 * r, width), F32),
            pltpu.VMEM((2 * r, width), F32),
            pltpu.VMEM((3 * r, 3 * r), F32),
            pltpu.SemaphoreType.DMA((ITERS, deep)),
            pltpu.SemaphoreType.DMA((ITERS, deep, wide)),
            pltpu.SemaphoreType.DMA((ITERS, deep, wide)),
            pltpu.SemaphoreType.DMA((ITERS, n)),
            pltpu.SemaphoreType.DMA((n,)),
            pltpu.SemaphoreType.DMA((n,)),
        ],
        compiler_params=pltpu.CompilerParams(
            collective_id=0, has_side_effects=True, vmem_limit_bytes=56 * 1024 * 1024
        ),
    )(points, lengthscales[None, :], noise[None, :], targets)


def solution(mesh):
    wide = P(None, ("groups", "pts"))
    return jax.shard_map(
        functools.partial(body, mesh.shape["pts"]),
        mesh=mesh,
        in_specs=(wide, P(), P(("groups", "pts")), wide),
        out_specs=(wide, wide),
        check_vma=False,
    )
```

```python
import functools

import jax
import jax.numpy as jnp
from jax import lax
from jax.experimental import pallas as pl
from jax.experimental.pallas import tpu as pltpu
from jax.sharding import PartitionSpec as P

ITERS = 3
MESH = pl.DeviceIdType.MESH
NT = (((1,), (1,)), ((), ()))
NN = (((1,), (0,)), ((), ()))
F32 = jnp.float32
BF16 = jnp.bfloat16


def mxu(left, right, dims):
    return lax.dot_general(left, right, dims, preferred_element_type=F32)


def split3(x):
    hi = x.astype(BF16)
    rest = x - hi.astype(F32)
    mid = rest.astype(BF16)
    low = (rest - mid.astype(F32)).astype(BF16)
    return hi, mid, low


def stack3(x):
    return jnp.concatenate(split3(x), axis=0)


def six_rows(stacked, rows):
    return jnp.concatenate([stacked, stacked[: 2 * rows], stacked[:rows]], axis=0)


def six_lanes(x):
    hi, mid, low = split3(x)
    wide = [hi, hi, hi, mid, mid, low]
    return jnp.concatenate([w.astype(F32) for w in wide], axis=1).astype(BF16)


def fold_gram(g, rows):
    r = rows
    total = g[2 * r :, :r] + g[r : 2 * r, r : 2 * r] + g[:r, 2 * r :]
    total = total + (g[r : 2 * r, :r] + g[:r, r : 2 * r])
    total = total + g[:r, :r]
    return 0.5 * (total + total.T)


def eliminate(systems, size):
    rows = lax.broadcasted_iota(jnp.int32, systems[0].shape, 0)
    for j in range(0, size, 2):
        i = j + 1
        done = []
        for m in systems:
            left = jnp.broadcast_to(m[:, j : j + 1], m.shape)
            right = jnp.broadcast_to(m[:, i : i + 1], m.shape)
            first, second = m[j : j + 1, :], m[i : i + 1, :]
            inv = 1.0 / left[j : j + 1, :]
            ratio = right[j : j + 1, :] * inv
            below = left[i : i + 1, :]
            schur = right[i : i + 1, :] - below * ratio
            second = (second - below * (first * inv)) / schur
            first = first * inv - ratio * second
            m = m - (left * first + right * second)
            done.append(jnp.where(rows == j, first, jnp.where(rows == i, second, m)))
        systems = done
    return [m[:, size : 2 * size] for m in systems]


def augmented(matrix, right):
    rows, size = matrix.shape
    pad = jnp.zeros((rows, 128 - 2 * size), F32)
    return jnp.concatenate([matrix, right, pad], axis=1)


def matern_tile(own, own_norm, feats):
    cross = mxu(own, six_rows(stack3(feats), feats.shape[0]), NN)
    norm = jnp.sum(feats * feats, axis=0, keepdims=True)
    d2 = own_norm + norm - 2.0 * cross
    x = jnp.maximum(5.0 * d2, 1e-30)
    t = x * lax.rsqrt(x)
    return (1.0 + t + x * (1.0 / 3.0)) * jnp.exp(-t)


def kernel(
    n, wide, pts_ref, ls_ref, noise_ref, tgt_ref, sol_ref, res_ref,
    gbuf, qbuf, pbuf, kth, ktl, dst, qst, rbuf, own_t, own_n, q_own, q_old,
    acc_h, acc_l, gram,
    send_z, send_y, send_k, recv, send_p, recv_p,
):
    me = lax.axis_index("pts")
    chips = n // 2
    deep = chips // wide
    chip = me // 2
    core = lax.rem(me, 2)
    sibling = 2 * chip + 1 - core
    z, y = chip // wide, lax.rem(chip, wide)

    def device(dz, dy):
        return 2 * (lax.rem(z + dz, deep) * wide + lax.rem(y + dy, wide)) + core
    f, width = pts_ref.shape
    r = tgt_ref.shape[0]

    barrier = pltpu.get_barrier_semaphore()

    def greet(s, c):
        peer = lax.rem(me + s, n)
        pl.semaphore_signal(barrier, inc=1, device_id={"pts": peer}, device_id_type=MESH)
        return c

    lax.fori_loop(1, n, greet, 0)

    scaled = pts_ref[...] / jnp.broadcast_to(ls_ref[...], (f, f)).T[:, :1]
    gbuf[me, :f, :] = scaled
    gbuf[me, f:, :] = tgt_ref[...]
    scaled_t = scaled.T
    own_t[...] = six_lanes(scaled_t)
    own_n[...] = jnp.broadcast_to(jnp.sum(scaled_t * scaled_t, axis=1, keepdims=True), own_n.shape)

    pl.semaphore_wait(barrier, n - 1)

    def to(rnd, buf, slot, peer, send):
        return pltpu.make_async_remote_copy(
            src_ref=buf.at[slot], dst_ref=buf.at[slot],
            send_sem=send, recv_sem=recv.at[rnd, slot],
            device_id={"pts": peer}, device_id_type=MESH,
        )

    def along_z(rnd, buf, dz):
        return to(rnd, buf, me, device(dz, 0), send_z.at[rnd, dz])

    def along_y(rnd, buf, dz, dy):
        return to(rnd, buf, device(deep - dz, 0), device(0, dy), send_y.at[rnd, dz, dy])

    def across(rnd, buf, dz, dy):
        slot = device(deep - dz, wide - dy)
        return to(rnd, buf, slot, sibling, send_k.at[rnd, dz, dy])

    def loop(begin, end, one):
        def run(s, c):
            one(s)
            return c

        lax.fori_loop(begin, end, run, 0)

    def gather_start(rnd, buf):
        loop(1, deep, lambda dz: along_z(rnd, buf, dz).start())
        for dy in range(1, wide):
            along_y(rnd, buf, 0, dy).start()
        across(rnd, buf, 0, 0).start()

    def gather_use(rnd, buf, use, batch, after_first=None):
        late = after_first is not None
        if not late:
            use([me])

        def use_line(dy):
            loop(0, deep // batch, lambda s: use([device(deep - s * batch - i, wide - dy) for i in range(batch)]))

        def lane(dz):
            copy = across(rnd, buf, dz, 0)
            copy.wait_recv()
            for dy in range(1, wide):
                along_y(rnd, buf, dz, dy).start()
            copy.start()
            if not late:
                use([device(deep - dz, 0)])

        loop(1, deep, lane)
        if late:
            after_first()
            use_line(0)
        for dy in range(1, wide):

            def plane(dz, dy=dy):
                copy = across(rnd, buf, dz, dy)
                copy.wait_recv()
                copy.start()
                if not late:
                    use([device(deep - dz, wide - dy)])

            loop(0, deep, plane)
            if late:
                use_line(dy)

        def other(s):
            slots = []
            for i in range(batch):
                at = s * batch + i
                slot = 2 * (lax.rem(z + deep - at // wide, deep) * wide + lax.rem(y + lax.rem(at, wide), wide)) + 1 - core
                to(rnd, buf, slot, sibling, send_k.at[rnd, 0, 0]).wait_recv()
                slots.append(slot)
            use(slots)

        loop(0, chips // batch, other)

    def lanes(parts):
        return parts[0] if len(parts) == 1 else jnp.concatenate(parts, axis=1)

    gather_start(0, gbuf)
    acc_h[...] = jnp.zeros_like(acc_h)
    acc_l[...] = jnp.zeros_like(acc_l)
    gram[...] = jnp.zeros_like(gram)

    def first(slots):
        stacks, highs, lows, values = [], [], [], [gbuf[slot, f:, :] for slot in slots]
        for slot, value in zip(slots, values):
            tile = matern_tile(own_t[...], own_n[...], gbuf[slot, :f, :])
            highs.append(tile.astype(BF16))
            lows.append((tile - highs[-1].astype(F32)).astype(BF16))
            stacks.append(stack3(value))
        stacked = lanes(stacks)
        gram[...] += mxu(stacked, stacked, NT)
        acc_h[...] += mxu(stacked, lanes(highs), NT)
        acc_l[...] += mxu(stacked[: 2 * r], lanes(lows), NT)
        for slot, value, high, low, stack in zip(slots, values, highs, lows, stacks):
            kth[slot] = high
            ktl[slot] = low
            rbuf[slot] = value
            dst[slot] = stack

    gather_use(0, gbuf, first, 2)
    rr = fold_gram(gram[...], r)
    eye = (
        lax.broadcasted_iota(jnp.int32, (r, r), 0) == lax.broadcasted_iota(jnp.int32, (r, r), 1)
    ).astype(F32)

    def operator(own):
        h = acc_h[...]
        l = acc_l[...]
        return (h[2 * r :] + l[r:]) + (h[r : 2 * r] + l[:r]) + h[:r] + noise_ref[...] * own

    solution = jnp.zeros((r, width), F32)
    image_r = operator(tgt_ref[...])
    qbuf[0, me] = image_r
    gather_start(1, qbuf.at[0])
    for step in range(ITERS - 1):
        buf = qbuf.at[step]
        beta_t = None if step == 0 else beta_t

        def directions(s, beta_t=beta_t):
            slots = [s * 4 + i for i in range(4)]
            value = lanes([rbuf[slot] for slot in slots]) + mxu(
                beta_t, six_rows(lanes([dst[slot] for slot in slots]), r), NN
            )
            stacked = stack3(value)
            for i, slot in enumerate(slots):
                dst[slot] = stacked[:, i * width : (i + 1) * width]

        def advance(step=step, directions=directions):
            if step > 0:
                loop(0, n // 4, directions)

        gram[...] = jnp.zeros_like(gram)
        acc_h[...] = jnp.zeros_like(acc_h)
        acc_l[...] = jnp.zeros_like(acc_l)

        def curvature(slots, buf=buf, beta_t=beta_t):
            value = lanes([buf[slot] for slot in slots])
            if beta_t is not None:
                value = value + mxu(beta_t, six_rows(lanes([qst[slot] for slot in slots]), r), NN)
            stacked = stack3(value)
            gram[...] += mxu(lanes([dst[slot] for slot in slots]), stacked, NT)
            acc_h[...] += mxu(stacked, lanes([kth[slot] for slot in slots]), NT)
            acc_l[...] += mxu(stacked[: 2 * r], lanes([ktl[slot] for slot in slots]), NT)
            for i, slot in enumerate(slots):
                qst[slot] = stacked[:, i * width : (i + 1) * width]

        gather_use(step + 1, buf, curvature, 4, advance)
        alpha, rr_inv = eliminate(
            [augmented(fold_gram(gram[...], r), rr), augmented(rr, eye)], r
        )
        alpha_t = six_lanes(alpha.T)
        solution = solution + mxu(alpha_t, six_rows(dst[me], r), NN)
        image = image_r
        if step > 0:
            image = image_r + mxu(beta_t, six_rows(q_old[...], r), NN)
        image_q = operator(image)
        image_r = image_r - mxu(alpha_t, six_rows(stack3(image_q), r), NN)
        if step + 2 < ITERS:
            qbuf[step + 1, me] = image_r
            gather_start(step + 2, qbuf.at[step + 1])
            q_old[...] = qst[me]
        gram[...] = jnp.zeros_like(gram)

        def residuals(s, alpha_t=alpha_t):
            slots = [s * 4 + i for i in range(4)]
            value = lanes([rbuf[slot] for slot in slots]) - mxu(
                alpha_t, six_rows(lanes([qst[slot] for slot in slots]), r), NN
            )
            stacked = stack3(value)
            gram[...] += mxu(stacked, stacked, NT)
            for i, slot in enumerate(slots):
                rbuf[slot] = value[:, i * width : (i + 1) * width]

        loop(0, n // 4, residuals)
        rr_next = fold_gram(gram[...], r)
        beta = jnp.dot(rr_inv, rr_next, precision=lax.Precision.HIGHEST, preferred_element_type=F32)
        beta_t = six_lanes(beta.T)
        q_own[...] = image_r + mxu(beta_t, six_rows(qst[me], r), NN)
        rr = rr_next

    dst[me] = stack3(rbuf[me] + mxu(beta_t, six_rows(dst[me], r), NN))
    q_stacked = stack3(q_own[...])
    g = mxu(dst[me], q_stacked, NT)
    partial = fold_gram(g, r)
    piece = pbuf.shape[1]
    pbuf[me] = jnp.concatenate([partial[i : i + piece] for i in range(0, r, piece)], axis=1)

    def to_peer(s, slot):
        return pltpu.make_async_remote_copy(
            src_ref=pbuf.at[slot], dst_ref=pbuf.at[slot],
            send_sem=send_p.at[s], recv_sem=recv_p.at[slot],
            device_id={"pts": lax.rem(me + s, n)}, device_id_type=MESH,
        )

    def give(s, c):
        to_peer(s, me).start()
        return c

    lax.fori_loop(1, n, give, 0)

    def take(s, c):
        to_peer(s, lax.rem(me + n - s, n)).wait_recv()
        return c

    lax.fori_loop(1, n, take, 0)
    total = lax.fori_loop(0, n, lambda s, c: c + pbuf[s], jnp.zeros((piece, 128), F32))
    total = jnp.concatenate([total[:, i : i + r] for i in range(0, 128, r)], axis=0)
    (alpha,) = eliminate([augmented(total, rr)], r)
    alpha_t = six_lanes(alpha.T)
    sol_ref[...] = solution + mxu(alpha_t, six_rows(dst[me], r), NN)
    res_ref[...] = rbuf[me] - mxu(alpha_t, six_rows(q_stacked, r), NN)

    for rnd in range(ITERS):
        buf = gbuf if rnd == 0 else qbuf.at[rnd - 1]

        def drain(dz, rnd=rnd, buf=buf):
            for dy in range(wide):
                if dy > 0:
                    along_y(rnd, buf, dz, dy).wait_send()
                across(rnd, buf, dz, dy).wait_send()

        loop(0, deep, drain)
        loop(1, deep, lambda dz, rnd=rnd, buf=buf: along_z(rnd, buf, dz).wait_send())

    def drain_peer(s, c):
        to_peer(s, me).wait_send()
        return c

    lax.fori_loop(1, n, drain_peer, 0)


def body(n, points, lengthscales, noise, targets):
    f, width = points.shape
    r = targets.shape[0]
    block = jax.ShapeDtypeStruct((r, width), F32)
    chips = n // 2
    wide = 2 if chips % 2 == 0 and chips <= 8 else 1
    deep = chips // wide
    vmem = pl.BlockSpec(memory_space=pltpu.VMEM)
    return pl.pallas_call(
        functools.partial(kernel, n, wide),
        out_shape=(block, block),
        in_specs=[vmem] * 4,
        out_specs=(vmem, vmem),
        scratch_shapes=[
            pltpu.VMEM((n, f + r, width), F32),
            pltpu.VMEM((ITERS - 1, n, r, width), F32),
            pltpu.VMEM((n, r * r // 128, 128), F32),
            pltpu.VMEM((n, width, width), BF16),
            pltpu.VMEM((n, width, width), BF16),
            pltpu.VMEM((n, 3 * r, width), BF16),
            pltpu.VMEM((n, 3 * r, width), BF16),
            pltpu.VMEM((n, r, width), F32),
            pltpu.VMEM((width, 6 * f), BF16),
            pltpu.VMEM((width, width), F32),
            pltpu.VMEM((r, width), F32),
            pltpu.VMEM((3 * r, width), BF16),
            pltpu.VMEM((3 * r, width), F32),
            pltpu.VMEM((2 * r, width), F32),
            pltpu.VMEM((3 * r, 3 * r), F32),
            pltpu.SemaphoreType.DMA((ITERS, deep)),
            pltpu.SemaphoreType.DMA((ITERS, deep, wide)),
            pltpu.SemaphoreType.DMA((ITERS, deep, wide)),
            pltpu.SemaphoreType.DMA((ITERS, n)),
            pltpu.SemaphoreType.DMA((n,)),
            pltpu.SemaphoreType.DMA((n,)),
        ],
        compiler_params=pltpu.CompilerParams(
            collective_id=0, has_side_effects=True, vmem_limit_bytes=56 * 1024 * 1024
        ),
    )(points, lengthscales[None, :], noise[None, :], targets)


def solution(mesh):
    wide = P(None, ("groups", "pts"))
    return jax.shard_map(
        functools.partial(body, mesh.shape["pts"]),
        mesh=mesh,
        in_specs=(wide, P(), P(("groups", "pts")), wide),
        out_specs=(wide, wide),
        check_vma=False,
    )
```

```python
import functools

import jax
import jax.numpy as jnp
from jax import lax
from jax.experimental import pallas as pl
from jax.experimental.pallas import tpu as pltpu
from jax.sharding import PartitionSpec as P

ITERS = 3
MESH = pl.DeviceIdType.MESH
NT = (((1,), (1,)), ((), ()))
NN = (((1,), (0,)), ((), ()))
F32 = jnp.float32
BF16 = jnp.bfloat16


def mxu(left, right, dims):
    return lax.dot_general(left, right, dims, preferred_element_type=F32)


def split3(x):
    hi = x.astype(BF16)
    rest = x - hi.astype(F32)
    mid = rest.astype(BF16)
    low = (rest - mid.astype(F32)).astype(BF16)
    return hi, mid, low


def stack3(x):
    return jnp.concatenate(split3(x), axis=0)


def six_rows(stacked, rows):
    return jnp.concatenate([stacked, stacked[: 2 * rows], stacked[:rows]], axis=0)


def six_lanes(x):
    hi, mid, low = split3(x)
    wide = [hi, hi, hi, mid, mid, low]
    return jnp.concatenate([w.astype(F32) for w in wide], axis=1).astype(BF16)


def fold_gram(g, rows):
    r = rows
    total = g[2 * r :, :r] + g[r : 2 * r, r : 2 * r] + g[:r, 2 * r :]
    total = total + (g[r : 2 * r, :r] + g[:r, r : 2 * r])
    total = total + g[:r, :r]
    return 0.5 * (total + total.T)


def eliminate(systems, size):
    rows = lax.broadcasted_iota(jnp.int32, systems[0].shape, 0)
    for j in range(0, size, 2):
        i = j + 1
        done = []
        for m in systems:
            left = jnp.broadcast_to(m[:, j : j + 1], m.shape)
            right = jnp.broadcast_to(m[:, i : i + 1], m.shape)
            first, second = m[j : j + 1, :], m[i : i + 1, :]
            inv = 1.0 / left[j : j + 1, :]
            ratio = right[j : j + 1, :] * inv
            below = left[i : i + 1, :]
            schur = right[i : i + 1, :] - below * ratio
            second = (second - below * (first * inv)) / schur
            first = first * inv - ratio * second
            m = m - (left * first + right * second)
            done.append(jnp.where(rows == j, first, jnp.where(rows == i, second, m)))
        systems = done
    return [m[:, size : 2 * size] for m in systems]


def augmented(matrix, right):
    rows, size = matrix.shape
    pad = jnp.zeros((rows, 128 - 2 * size), F32)
    return jnp.concatenate([matrix, right, pad], axis=1)


def matern_tile(own, own_norm, feats):
    cross = mxu(own, six_rows(stack3(feats), feats.shape[0]), NN)
    norm = jnp.sum(feats * feats, axis=0, keepdims=True)
    d2 = own_norm + norm - 2.0 * cross
    x = jnp.maximum(5.0 * d2, 1e-30)
    t = x * lax.rsqrt(x)
    return (1.0 + t + x * (1.0 / 3.0)) * jnp.exp(-t)


def kernel(
    n, wide, pts_ref, ls_ref, noise_ref, tgt_ref, out_ref,
    gbuf, qbuf, pbuf, kth, ktl, dst, qst, rbuf, own_t, own_n, q_own, q_old,
    acc_h, acc_l, gram,
    send_z, send_y, send_k, recv, send_p, recv_p,
):
    me = lax.axis_index("pts")
    chips = n // 2
    deep = chips // wide
    chip = me // 2
    core = lax.rem(me, 2)
    sibling = 2 * chip + 1 - core
    z, y = chip // wide, lax.rem(chip, wide)

    def device(dz, dy):
        return 2 * (lax.rem(z + dz, deep) * wide + lax.rem(y + dy, wide)) + core
    f, width = pts_ref.shape
    r = tgt_ref.shape[0]

    barrier = pltpu.get_barrier_semaphore()

    def greet(s, c):
        peer = lax.rem(me + s, n)
        pl.semaphore_signal(barrier, inc=1, device_id={"pts": peer}, device_id_type=MESH)
        return c

    lax.fori_loop(1, n, greet, 0)

    scaled = pts_ref[...] / jnp.broadcast_to(ls_ref[...], (f, f)).T[:, :1]
    gbuf[me, :f, :] = scaled
    gbuf[me, f:, :] = tgt_ref[...]
    scaled_t = scaled.T
    own_t[...] = six_lanes(scaled_t)
    own_n[...] = jnp.broadcast_to(jnp.sum(scaled_t * scaled_t, axis=1, keepdims=True), own_n.shape)

    pl.semaphore_wait(barrier, n - 1)

    def to(rnd, buf, slot, peer, send):
        return pltpu.make_async_remote_copy(
            src_ref=buf.at[slot], dst_ref=buf.at[slot],
            send_sem=send, recv_sem=recv.at[rnd, slot],
            device_id={"pts": peer}, device_id_type=MESH,
        )

    def along_z(rnd, buf, dz):
        return to(rnd, buf, me, device(dz, 0), send_z.at[rnd, dz])

    def along_y(rnd, buf, dz, dy):
        return to(rnd, buf, device(deep - dz, 0), device(0, dy), send_y.at[rnd, dz, dy])

    def across(rnd, buf, dz, dy):
        slot = device(deep - dz, wide - dy)
        return to(rnd, buf, slot, sibling, send_k.at[rnd, dz, dy])

    def loop(begin, end, one):
        def run(s, c):
            one(s)
            return c

        lax.fori_loop(begin, end, run, 0)

    def gather_start(rnd, buf):
        loop(1, deep, lambda dz: along_z(rnd, buf, dz).start())
        for dy in range(1, wide):
            along_y(rnd, buf, 0, dy).start()
        across(rnd, buf, 0, 0).start()

    def gather_use(rnd, buf, use, batch, after_first=None):
        late = after_first is not None
        if not late:
            use([me])

        def use_line(dy):
            loop(0, deep // batch, lambda s: use([device(deep - s * batch - i, wide - dy) for i in range(batch)]))

        def lane(dz):
            copy = across(rnd, buf, dz, 0)
            copy.wait_recv()
            for dy in range(1, wide):
                along_y(rnd, buf, dz, dy).start()
            copy.start()
            if not late:
                use([device(deep - dz, 0)])

        loop(1, deep, lane)
        if late:
            after_first()
            use_line(0)
        for dy in range(1, wide):

            def plane(dz, dy=dy):
                copy = across(rnd, buf, dz, dy)
                copy.wait_recv()
                copy.start()
                if not late:
                    use([device(deep - dz, wide - dy)])

            loop(0, deep, plane)
            if late:
                use_line(dy)

        def other(s):
            slots = []
            for i in range(batch):
                at = s * batch + i
                slot = 2 * (lax.rem(z + deep - at // wide, deep) * wide + lax.rem(y + lax.rem(at, wide), wide)) + 1 - core
                to(rnd, buf, slot, sibling, send_k.at[rnd, 0, 0]).wait_recv()
                slots.append(slot)
            use(slots)

        loop(0, chips // batch, other)

    def lanes(parts):
        return parts[0] if len(parts) == 1 else jnp.concatenate(parts, axis=1)

    gather_start(0, gbuf)
    acc_h[...] = jnp.zeros_like(acc_h)
    acc_l[...] = jnp.zeros_like(acc_l)
    gram[...] = jnp.zeros_like(gram)

    def first(slots):
        stacks, highs, lows, values = [], [], [], [gbuf[slot, f:, :] for slot in slots]
        for slot, value in zip(slots, values):
            tile = matern_tile(own_t[...], own_n[...], gbuf[slot, :f, :])
            highs.append(tile.astype(BF16))
            lows.append((tile - highs[-1].astype(F32)).astype(BF16))
            stacks.append(stack3(value))
        stacked = lanes(stacks)
        gram[...] += mxu(stacked, stacked, NT)
        acc_h[...] += mxu(stacked, lanes(highs), NT)
        acc_l[...] += mxu(stacked[: 2 * r], lanes(lows), NT)
        for slot, value, high, low, stack in zip(slots, values, highs, lows, stacks):
            kth[slot] = high
            ktl[slot] = low
            rbuf[slot] = value
            dst[slot] = stack

    gather_use(0, gbuf, first, 2)
    rr = fold_gram(gram[...], r)
    eye = (
        lax.broadcasted_iota(jnp.int32, (r, r), 0) == lax.broadcasted_iota(jnp.int32, (r, r), 1)
    ).astype(F32)

    def operator(own):
        h = acc_h[...]
        l = acc_l[...]
        return (h[2 * r :] + l[r:]) + (h[r : 2 * r] + l[:r]) + h[:r] + noise_ref[...] * own

    solution = jnp.zeros((r, width), F32)
    image_r = operator(tgt_ref[...])
    qbuf[0, me] = image_r
    gather_start(1, qbuf.at[0])
    for step in range(ITERS - 1):
        buf = qbuf.at[step]
        beta_t = None if step == 0 else beta_t

        def directions(s, beta_t=beta_t):
            slots = [s * 4 + i for i in range(4)]
            value = lanes([rbuf[slot] for slot in slots]) + mxu(
                beta_t, six_rows(lanes([dst[slot] for slot in slots]), r), NN
            )
            stacked = stack3(value)
            for i, slot in enumerate(slots):
                dst[slot] = stacked[:, i * width : (i + 1) * width]

        def advance(step=step, directions=directions):
            if step > 0:
                loop(0, n // 4, directions)

        gram[...] = jnp.zeros_like(gram)
        acc_h[...] = jnp.zeros_like(acc_h)
        acc_l[...] = jnp.zeros_like(acc_l)

        def curvature(slots, buf=buf, beta_t=beta_t):
            value = lanes([buf[slot] for slot in slots])
            if beta_t is not None:
                value = value + mxu(beta_t, six_rows(lanes([qst[slot] for slot in slots]), r), NN)
            stacked = stack3(value)
            gram[...] += mxu(lanes([dst[slot] for slot in slots]), stacked, NT)
            acc_h[...] += mxu(stacked, lanes([kth[slot] for slot in slots]), NT)
            acc_l[...] += mxu(stacked[: 2 * r], lanes([ktl[slot] for slot in slots]), NT)
            for i, slot in enumerate(slots):
                qst[slot] = stacked[:, i * width : (i + 1) * width]

        gather_use(step + 1, buf, curvature, 4, advance)
        alpha, rr_inv = eliminate(
            [augmented(fold_gram(gram[...], r), rr), augmented(rr, eye)], r
        )
        alpha_t = six_lanes(alpha.T)
        solution = solution + mxu(alpha_t, six_rows(dst[me], r), NN)
        image = image_r
        if step > 0:
            image = image_r + mxu(beta_t, six_rows(q_old[...], r), NN)
        image_q = operator(image)
        image_r = image_r - mxu(alpha_t, six_rows(stack3(image_q), r), NN)
        if step + 2 < ITERS:
            qbuf[step + 1, me] = image_r
            gather_start(step + 2, qbuf.at[step + 1])
            q_old[...] = qst[me]
        gram[...] = jnp.zeros_like(gram)

        def residuals(s, alpha_t=alpha_t):
            slots = [s * 4 + i for i in range(4)]
            value = lanes([rbuf[slot] for slot in slots]) - mxu(
                alpha_t, six_rows(lanes([qst[slot] for slot in slots]), r), NN
            )
            stacked = stack3(value)
            gram[...] += mxu(stacked, stacked, NT)
            for i, slot in enumerate(slots):
                rbuf[slot] = value[:, i * width : (i + 1) * width]

        loop(0, n // 4, residuals)
        rr_next = fold_gram(gram[...], r)
        beta = jnp.dot(rr_inv, rr_next, precision=lax.Precision.HIGHEST, preferred_element_type=F32)
        beta_t = six_lanes(beta.T)
        q_own[...] = image_r + mxu(beta_t, six_rows(qst[me], r), NN)
        rr = rr_next

    dst[me] = stack3(rbuf[me] + mxu(beta_t, six_rows(dst[me], r), NN))
    q_stacked = stack3(q_own[...])
    g = mxu(dst[me], q_stacked, NT)
    partial = fold_gram(g, r)
    piece = pbuf.shape[1]
    pbuf[me] = jnp.concatenate([partial[i : i + piece] for i in range(0, r, piece)], axis=1)

    def to_peer(s, slot):
        return pltpu.make_async_remote_copy(
            src_ref=pbuf.at[slot], dst_ref=pbuf.at[slot],
            send_sem=send_p.at[s], recv_sem=recv_p.at[slot],
            device_id={"pts": lax.rem(me + s, n)}, device_id_type=MESH,
        )

    def give(s, c):
        to_peer(s, me).start()
        return c

    lax.fori_loop(1, n, give, 0)

    def take(s, c):
        to_peer(s, lax.rem(me + n - s, n)).wait_recv()
        return c

    lax.fori_loop(1, n, take, 0)
    total = lax.fori_loop(0, n, lambda s, c: c + pbuf[s], jnp.zeros((piece, 128), F32))
    total = jnp.concatenate([total[:, i : i + r] for i in range(0, 128, r)], axis=0)
    (alpha,) = eliminate([augmented(total, rr)], r)
    alpha_t = six_lanes(alpha.T)
    out_ref[:r, :] = solution + mxu(alpha_t, six_rows(dst[me], r), NN)
    out_ref[r:, :] = rbuf[me] - mxu(alpha_t, six_rows(q_stacked, r), NN)

    for rnd in range(ITERS):
        buf = gbuf if rnd == 0 else qbuf.at[rnd - 1]

        def drain(dz, rnd=rnd, buf=buf):
            for dy in range(wide):
                if dy > 0:
                    along_y(rnd, buf, dz, dy).wait_send()
                across(rnd, buf, dz, dy).wait_send()

        loop(0, deep, drain)
        loop(1, deep, lambda dz, rnd=rnd, buf=buf: along_z(rnd, buf, dz).wait_send())

    def drain_peer(s, c):
        to_peer(s, me).wait_send()
        return c

    lax.fori_loop(1, n, drain_peer, 0)


def body(n, points, lengthscales, noise, targets):
    f, width = points.shape
    r = targets.shape[0]
    block = jax.ShapeDtypeStruct((2 * r, width), F32)
    chips = n // 2
    wide = 2 if chips % 2 == 0 and chips <= 8 else 1
    deep = chips // wide
    vmem = pl.BlockSpec(memory_space=pltpu.VMEM)
    out = pl.pallas_call(
        functools.partial(kernel, n, wide),
        out_shape=block,
        in_specs=[vmem] * 4,
        out_specs=vmem,
        scratch_shapes=[
            pltpu.VMEM((n, f + r, width), F32),
            pltpu.VMEM((ITERS - 1, n, r, width), F32),
            pltpu.VMEM((n, r * r // 128, 128), F32),
            pltpu.VMEM((n, width, width), BF16),
            pltpu.VMEM((n, width, width), BF16),
            pltpu.VMEM((n, 3 * r, width), BF16),
            pltpu.VMEM((n, 3 * r, width), BF16),
            pltpu.VMEM((n, r, width), F32),
            pltpu.VMEM((width, 6 * f), BF16),
            pltpu.VMEM((width, width), F32),
            pltpu.VMEM((r, width), F32),
            pltpu.VMEM((3 * r, width), BF16),
            pltpu.VMEM((3 * r, width), F32),
            pltpu.VMEM((2 * r, width), F32),
            pltpu.VMEM((3 * r, 3 * r), F32),
            pltpu.SemaphoreType.DMA((ITERS, deep)),
            pltpu.SemaphoreType.DMA((ITERS, deep, wide)),
            pltpu.SemaphoreType.DMA((ITERS, deep, wide)),
            pltpu.SemaphoreType.DMA((ITERS, n)),
            pltpu.SemaphoreType.DMA((n,)),
            pltpu.SemaphoreType.DMA((n,)),
        ],
        compiler_params=pltpu.CompilerParams(
            collective_id=0, has_side_effects=True, vmem_limit_bytes=56 * 1024 * 1024
        ),
    )(points, lengthscales[None, :], noise[None, :], targets)
    return out[:r], out[r:]


def solution(mesh):
    wide = P(None, ("groups", "pts"))
    return jax.shard_map(
        functools.partial(body, mesh.shape["pts"]),
        mesh=mesh,
        in_specs=(wide, P(), P(("groups", "pts")), wide),
        out_specs=(wide, wide),
        check_vma=False,
    )
```

```python
import functools

import jax
import jax.numpy as jnp
from jax import lax
from jax.experimental import pallas as pl
from jax.experimental.pallas import tpu as pltpu
from jax.sharding import PartitionSpec as P

ITERS = 3
MESH = pl.DeviceIdType.MESH
NT = (((1,), (1,)), ((), ()))
NN = (((1,), (0,)), ((), ()))
F32 = jnp.float32
BF16 = jnp.bfloat16


def mxu(left, right, dims):
    return lax.dot_general(left, right, dims, preferred_element_type=F32)


def split3(x):
    hi = x.astype(BF16)
    rest = x - hi.astype(F32)
    mid = rest.astype(BF16)
    low = (rest - mid.astype(F32)).astype(BF16)
    return hi, mid, low


def stack3(x):
    return jnp.concatenate(split3(x), axis=0)


def six_rows(stacked, rows):
    return jnp.concatenate([stacked, stacked[: 2 * rows], stacked[:rows]], axis=0)


def six_lanes(x):
    hi, mid, low = split3(x)
    wide = [hi, hi, hi, mid, mid, low]
    return jnp.concatenate([w.astype(F32) for w in wide], axis=1).astype(BF16)


def fold_gram(g, rows):
    r = rows
    total = g[2 * r :, :r] + g[r : 2 * r, r : 2 * r] + g[:r, 2 * r :]
    total = total + (g[r : 2 * r, :r] + g[:r, r : 2 * r])
    total = total + g[:r, :r]
    return 0.5 * (total + total.T)


def eliminate(systems, size):
    rows = lax.broadcasted_iota(jnp.int32, systems[0].shape, 0)
    for j in range(0, size, 2):
        i = j + 1
        done = []
        for m in systems:
            left = jnp.broadcast_to(m[:, j : j + 1], m.shape)
            right = jnp.broadcast_to(m[:, i : i + 1], m.shape)
            first, second = m[j : j + 1, :], m[i : i + 1, :]
            inv = 1.0 / left[j : j + 1, :]
            ratio = right[j : j + 1, :] * inv
            below = left[i : i + 1, :]
            schur = right[i : i + 1, :] - below * ratio
            second = (second - below * (first * inv)) / schur
            first = first * inv - ratio * second
            m = m - (left * first + right * second)
            done.append(jnp.where(rows == j, first, jnp.where(rows == i, second, m)))
        systems = done
    return [m[:, size : 2 * size] for m in systems]


def augmented(matrix, right):
    rows, size = matrix.shape
    pad = jnp.zeros((rows, 128 - 2 * size), F32)
    return jnp.concatenate([matrix, right, pad], axis=1)


def matern_tile(own, own_norm, feats):
    cross = mxu(own, six_rows(stack3(feats), feats.shape[0]), NN)
    norm = jnp.sum(feats * feats, axis=0, keepdims=True)
    d2 = own_norm + norm - 2.0 * cross
    x = jnp.maximum(5.0 * d2, 1e-30)
    t = x * lax.rsqrt(x)
    return (1.0 + t + x * (1.0 / 3.0)) * jnp.exp(-t)


def kernel(
    n, wide, pts_ref, ls_ref, noise_ref, tgt_ref, out_ref,
    gbuf, qbuf, pbuf, kth, ktl, dst, qst, rbuf, own_t, own_n, q_own, q_old,
    acc_h, acc_l, gram,
    send_z, send_y, send_k, recv, send_p, recv_p,
):
    me = lax.axis_index("pts")
    chips = n // 2
    deep = chips // wide
    chip = me // 2
    core = lax.rem(me, 2)
    sibling = 2 * chip + 1 - core
    z, y = chip // wide, lax.rem(chip, wide)

    def device(dz, dy):
        return 2 * (lax.rem(z + dz, deep) * wide + lax.rem(y + dy, wide)) + core
    f, width = pts_ref.shape
    r = tgt_ref.shape[0]

    barrier = pltpu.get_barrier_semaphore()

    def greet(s, c):
        peer = lax.rem(me + s, n)
        pl.semaphore_signal(barrier, inc=1, device_id={"pts": peer}, device_id_type=MESH)
        return c

    lax.fori_loop(1, n, greet, 0)

    scaled = pts_ref[...] / jnp.broadcast_to(ls_ref[...], (f, f)).T[:, :1]
    gbuf[me, :f, :] = scaled
    gbuf[me, f:, :] = tgt_ref[...]
    scaled_t = scaled.T
    own_t[...] = six_lanes(scaled_t)
    own_n[...] = jnp.broadcast_to(jnp.sum(scaled_t * scaled_t, axis=1, keepdims=True), own_n.shape)

    pl.semaphore_wait(barrier, n - 1)

    def to(rnd, buf, slot, peer, send):
        return pltpu.make_async_remote_copy(
            src_ref=buf.at[slot], dst_ref=buf.at[slot],
            send_sem=send, recv_sem=recv.at[rnd, slot],
            device_id={"pts": peer}, device_id_type=MESH,
        )

    def along_z(rnd, buf, dz):
        return to(rnd, buf, me, device(dz, 0), send_z.at[rnd, dz])

    def along_y(rnd, buf, dz, dy):
        return to(rnd, buf, device(deep - dz, 0), device(0, dy), send_y.at[rnd, dz, dy])

    def across(rnd, buf, dz, dy):
        slot = device(deep - dz, wide - dy)
        return to(rnd, buf, slot, sibling, send_k.at[rnd, dz, dy])

    def loop(begin, end, one):
        def run(s, c):
            one(s)
            return c

        lax.fori_loop(begin, end, run, 0)

    def gather_start(rnd, buf):
        loop(1, deep, lambda dz: along_z(rnd, buf, dz).start())
        for dy in range(1, wide):
            along_y(rnd, buf, 0, dy).start()
        across(rnd, buf, 0, 0).start()

    def gather_use(rnd, buf, use, batch, after_first=None):
        late = after_first is not None
        if not late:
            use([me])

        def use_line(dy):
            loop(0, deep // batch, lambda s: use([device(deep - s * batch - i, wide - dy) for i in range(batch)]))

        def lane(dz):
            copy = across(rnd, buf, dz, 0)
            copy.wait_recv()
            for dy in range(1, wide):
                along_y(rnd, buf, dz, dy).start()
            copy.start()
            if not late:
                use([device(deep - dz, 0)])

        loop(1, deep, lane)
        if late:
            after_first()
            use_line(0)
        for dy in range(1, wide):

            def plane(dz, dy=dy):
                copy = across(rnd, buf, dz, dy)
                copy.wait_recv()
                copy.start()
                if not late:
                    use([device(deep - dz, wide - dy)])

            loop(0, deep, plane)
            if late:
                use_line(dy)

        def other(s):
            slots = []
            for i in range(batch):
                at = s * batch + i
                slot = 2 * (lax.rem(z + deep - at // wide, deep) * wide + lax.rem(y + lax.rem(at, wide), wide)) + 1 - core
                to(rnd, buf, slot, sibling, send_k.at[rnd, 0, 0]).wait_recv()
                slots.append(slot)
            use(slots)

        loop(0, chips // batch, other)

    def lanes(parts):
        return parts[0] if len(parts) == 1 else jnp.concatenate(parts, axis=1)

    gather_start(0, gbuf)
    acc_h[...] = jnp.zeros_like(acc_h)
    acc_l[...] = jnp.zeros_like(acc_l)
    gram[...] = jnp.zeros_like(gram)

    def first(slots):
        stacks, highs, lows, values = [], [], [], [gbuf[slot, f:, :] for slot in slots]
        for slot, value in zip(slots, values):
            tile = matern_tile(own_t[...], own_n[...], gbuf[slot, :f, :])
            highs.append(tile.astype(BF16))
            lows.append((tile - highs[-1].astype(F32)).astype(BF16))
            stacks.append(stack3(value))
        stacked = lanes(stacks)
        gram[...] += mxu(stacked, stacked, NT)
        acc_h[...] += mxu(stacked, lanes(highs), NT)
        acc_l[...] += mxu(stacked[: 2 * r], lanes(lows), NT)
        for slot, value, high, low, stack in zip(slots, values, highs, lows, stacks):
            kth[slot] = high
            ktl[slot] = low
            rbuf[slot] = value
            dst[slot] = stack

    gather_use(0, gbuf, first, 2)
    rr = fold_gram(gram[...], r)
    eye = (
        lax.broadcasted_iota(jnp.int32, (r, r), 0) == lax.broadcasted_iota(jnp.int32, (r, r), 1)
    ).astype(F32)

    def operator(own):
        h = acc_h[...]
        l = acc_l[...]
        return (h[2 * r :] + l[r:]) + (h[r : 2 * r] + l[:r]) + h[:r] + noise_ref[...] * own

    solution = jnp.zeros((r, width), F32)
    image_r = operator(tgt_ref[...])
    qbuf[0, me] = image_r
    gather_start(1, qbuf.at[0])
    for step in range(ITERS - 1):
        buf = qbuf.at[step]
        beta_t = None if step == 0 else beta_t

        def directions(s, beta_t=beta_t):
            slots = [s * 8 + i for i in range(8)]
            value = lanes([rbuf[slot] for slot in slots]) + mxu(
                beta_t, six_rows(lanes([dst[slot] for slot in slots]), r), NN
            )
            stacked = stack3(value)
            for i, slot in enumerate(slots):
                dst[slot] = stacked[:, i * width : (i + 1) * width]

        def advance(step=step, directions=directions):
            if step > 0:
                loop(0, n // 8, directions)

        gram[...] = jnp.zeros_like(gram)
        acc_h[...] = jnp.zeros_like(acc_h)
        acc_l[...] = jnp.zeros_like(acc_l)

        def curvature(slots, buf=buf, beta_t=beta_t):
            value = lanes([buf[slot] for slot in slots])
            if beta_t is not None:
                value = value + mxu(beta_t, six_rows(lanes([qst[slot] for slot in slots]), r), NN)
            stacked = stack3(value)
            gram[...] += mxu(lanes([dst[slot] for slot in slots]), stacked, NT)
            acc_h[...] += mxu(stacked, lanes([kth[slot] for slot in slots]), NT)
            acc_l[...] += mxu(stacked[: 2 * r], lanes([ktl[slot] for slot in slots]), NT)
            for i, slot in enumerate(slots):
                qst[slot] = stacked[:, i * width : (i + 1) * width]

        gather_use(step + 1, buf, curvature, 4, advance)
        alpha, rr_inv = eliminate(
            [augmented(fold_gram(gram[...], r), rr), augmented(rr, eye)], r
        )
        alpha_t = six_lanes(alpha.T)
        solution = solution + mxu(alpha_t, six_rows(dst[me], r), NN)
        image = image_r
        if step > 0:
            image = image_r + mxu(beta_t, six_rows(q_old[...], r), NN)
        image_q = operator(image)
        image_r = image_r - mxu(alpha_t, six_rows(stack3(image_q), r), NN)
        if step + 2 < ITERS:
            qbuf[step + 1, me] = image_r
            gather_start(step + 2, qbuf.at[step + 1])
            q_old[...] = qst[me]
        gram[...] = jnp.zeros_like(gram)

        def residuals(s, alpha_t=alpha_t):
            slots = [s * 8 + i for i in range(8)]
            value = lanes([rbuf[slot] for slot in slots]) - mxu(
                alpha_t, six_rows(lanes([qst[slot] for slot in slots]), r), NN
            )
            stacked = stack3(value)
            gram[...] += mxu(stacked, stacked, NT)
            for i, slot in enumerate(slots):
                rbuf[slot] = value[:, i * width : (i + 1) * width]

        loop(0, n // 8, residuals)
        rr_next = fold_gram(gram[...], r)
        beta = jnp.dot(rr_inv, rr_next, precision=lax.Precision.HIGHEST, preferred_element_type=F32)
        beta_t = six_lanes(beta.T)
        q_own[...] = image_r + mxu(beta_t, six_rows(qst[me], r), NN)
        rr = rr_next

    dst[me] = stack3(rbuf[me] + mxu(beta_t, six_rows(dst[me], r), NN))
    q_stacked = stack3(q_own[...])
    g = mxu(dst[me], q_stacked, NT)
    partial = fold_gram(g, r)
    piece = pbuf.shape[1]
    pbuf[me] = jnp.concatenate([partial[i : i + piece] for i in range(0, r, piece)], axis=1)

    def to_peer(s, slot):
        return pltpu.make_async_remote_copy(
            src_ref=pbuf.at[slot], dst_ref=pbuf.at[slot],
            send_sem=send_p.at[s], recv_sem=recv_p.at[slot],
            device_id={"pts": lax.rem(me + s, n)}, device_id_type=MESH,
        )

    def give(s, c):
        to_peer(s, me).start()
        return c

    lax.fori_loop(1, n, give, 0)

    def take(s, c):
        to_peer(s, lax.rem(me + n - s, n)).wait_recv()
        return c

    lax.fori_loop(1, n, take, 0)
    total = lax.fori_loop(0, n, lambda s, c: c + pbuf[s], jnp.zeros((piece, 128), F32))
    total = jnp.concatenate([total[:, i : i + r] for i in range(0, 128, r)], axis=0)
    (alpha,) = eliminate([augmented(total, rr)], r)
    alpha_t = six_lanes(alpha.T)
    out_ref[:r, :] = solution + mxu(alpha_t, six_rows(dst[me], r), NN)
    out_ref[r:, :] = rbuf[me] - mxu(alpha_t, six_rows(q_stacked, r), NN)

    for rnd in range(ITERS):
        buf = gbuf if rnd == 0 else qbuf.at[rnd - 1]

        def drain(dz, rnd=rnd, buf=buf):
            for dy in range(wide):
                if dy > 0:
                    along_y(rnd, buf, dz, dy).wait_send()
                across(rnd, buf, dz, dy).wait_send()

        loop(0, deep, drain)
        loop(1, deep, lambda dz, rnd=rnd, buf=buf: along_z(rnd, buf, dz).wait_send())

    def drain_peer(s, c):
        to_peer(s, me).wait_send()
        return c

    lax.fori_loop(1, n, drain_peer, 0)


def body(n, points, lengthscales, noise, targets):
    f, width = points.shape
    r = targets.shape[0]
    block = jax.ShapeDtypeStruct((2 * r, width), F32)
    chips = n // 2
    wide = 2 if chips % 2 == 0 and chips <= 8 else 1
    deep = chips // wide
    vmem = pl.BlockSpec(memory_space=pltpu.VMEM)
    out = pl.pallas_call(
        functools.partial(kernel, n, wide),
        out_shape=block,
        in_specs=[vmem] * 4,
        out_specs=vmem,
        scratch_shapes=[
            pltpu.VMEM((n, f + r, width), F32),
            pltpu.VMEM((ITERS - 1, n, r, width), F32),
            pltpu.VMEM((n, r * r // 128, 128), F32),
            pltpu.VMEM((n, width, width), BF16),
            pltpu.VMEM((n, width, width), BF16),
            pltpu.VMEM((n, 3 * r, width), BF16),
            pltpu.VMEM((n, 3 * r, width), BF16),
            pltpu.VMEM((n, r, width), F32),
            pltpu.VMEM((width, 6 * f), BF16),
            pltpu.VMEM((width, width), F32),
            pltpu.VMEM((r, width), F32),
            pltpu.VMEM((3 * r, width), BF16),
            pltpu.VMEM((3 * r, width), F32),
            pltpu.VMEM((2 * r, width), F32),
            pltpu.VMEM((3 * r, 3 * r), F32),
            pltpu.SemaphoreType.DMA((ITERS, deep)),
            pltpu.SemaphoreType.DMA((ITERS, deep, wide)),
            pltpu.SemaphoreType.DMA((ITERS, deep, wide)),
            pltpu.SemaphoreType.DMA((ITERS, n)),
            pltpu.SemaphoreType.DMA((n,)),
            pltpu.SemaphoreType.DMA((n,)),
        ],
        compiler_params=pltpu.CompilerParams(
            collective_id=0, has_side_effects=True, vmem_limit_bytes=56 * 1024 * 1024
        ),
    )(points, lengthscales[None, :], noise[None, :], targets)
    return out[:r], out[r:]


def solution(mesh):
    wide = P(None, ("groups", "pts"))
    return jax.shard_map(
        functools.partial(body, mesh.shape["pts"]),
        mesh=mesh,
        in_specs=(wide, P(), P(("groups", "pts")), wide),
        out_specs=(wide, wide),
        check_vma=False,
    )
```
